32 devices in a mesh: groups: 2 (over y), col: 4 (over z), row: 2 (over x), rhs: 2 (over core).
Axes of the slice: x: 2, y: 2, z: 4, core: 2. Of those that a mesh axis runs over, the one named last changes fastest.
Arguments:
- prev_panel: float32 [4, 2048, 4096], P(None, 'row', 'col'), may hold values from -0.09375 to 0.09375
- lower_panel: float32 [3, 2048, 3, 2048], P(None, 'row', None, 'col'), may hold values from -0.125 to 0.125
- solved_prev: float32 [4096, 1024], P('col', ('groups', 'rhs')), parts along dimension 1, may hold values from -6 to 6
- right_block: float32 [8, 2048, 512], P('groups', 'row', 'rhs'), parts along dimension 0, may hold values from -6 to 6
- block_inverse: float32 [4, 2048, 2048], P(None, 'col', 'row'), may hold values from -1 to 1, as said below
Outputs:
- solved: float32 [8, 2048, 512], P('groups', 'col', 'rhs'), parts along dimension 0
The draws below stay inside these ranges and needn't reach their ends.
There are 2 independent parts, one for each index of `groups`. The reference program is written for one: setup_inputs(seed, part) draws one part's arguments, and reference() takes and returns one part's arrays. A program takes and returns all parts, laid end to end along the dimension named above; an argument that names none is the same for every part. Nothing has to cross between parts.
Inputs may be any that keep to these rules, and one draw needn't show every extreme that they name: Each block_inverse[k] is lower triangular with diagonal entries from 0.5 to 1.
All inputs are finite; a program needn't handle non-finite values.
Results may differ from the reference program's by a relative error of at most 0.0001.
Values sent between devices are 32-bit elements; how exact they have to be, the bound alone decides.
A program may use at most 128 MiB of HBM per device.

```python
import jax
import jax.numpy as jnp
from jax import lax

NB = 2048
NBLK = 4
M = 512
PREV = 4096


def draw_block_inverse(key, part):
    first_key, second_key = jax.random.split(jax.random.fold_in(key, 17))
    spread = jax.random.uniform(first_key, (NBLK, NB, NB), jnp.float32, -1.0, 1.0) * (0.9 / jnp.sqrt(jnp.float32(NB)))
    diagonal = jax.random.uniform(second_key, (NBLK, NB), jnp.float32, 0.5, 1.0)
    places = jnp.arange(NB)
    below = places[:, None] > places[None, :]
    same = places[:, None] == places[None, :]
    return jnp.where(below[None], spread, 0.0) + jnp.where(same[None], diagonal[:, :, None], 0.0)


def block_levels(stream_key, dims, cuts, least, top_value):
    factor_of, own = 1.0, jax.random.fold_in(stream_key, 6)
    for dim, parts in cuts:
        draws = jnp.exp(jax.random.uniform(jax.random.fold_in(own, dim), (parts,), jnp.float32, least / len(cuts), top_value / len(cuts)))
        factor_of = factor_of * jnp.repeat(draws, dims[dim] // parts).reshape([-1 if axis == dim else 1 for axis in range(len(dims))])
    return factor_of


def gaussian(key, shape, scale, most, cuts=(), kind=jnp.bfloat16):
    level = block_levels(key, shape, cuts, -0.22, 0.18) if cuts else 1.0
    drawn = jax.random.normal(key, shape, jnp.float32) * scale * level
    return jnp.minimum(jnp.maximum(drawn, -most), most).astype(kind)


def setup_inputs(seed: int = 0, part: int = 0) -> dict:
    key_list = jax.random.split(jax.random.key(seed), 6)
    own_keys = jax.random.split(jax.random.fold_in(key_list[5], part), 6)
    return {
        "prev_panel": gaussian(key_list[0], (NBLK, NB, PREV), PREV ** -0.5, 0.09375, ((1, 2), (2, 4)), jnp.float32),
        "lower_panel": gaussian(key_list[1], (NBLK - 1, NB, NBLK - 1, NB), NB ** -0.5, 0.125, ((1, 2), (3, 4)), jnp.float32),
        "solved_prev": gaussian(own_keys[2], (PREV, M), 1.0, 6.0, ((0, 4), (1, 2)), jnp.float32),
        "right_block": gaussian(own_keys[3], (NBLK, NB, M), 1.0, 6.0, ((1, 2), (2, 2)), jnp.float32),
        "block_inverse": draw_block_inverse(jax.random.fold_in(key_list[5], 71), part),
    }


def product(left, right):
    return jnp.dot(left, right, precision=lax.Precision.HIGHEST, preferred_element_type=jnp.float32)


def reference(prev_panel, lower_panel, solved_prev, right_block, block_inverse):
    solved = []
    for block in range(NBLK):
        partial_value = product(prev_panel[block], solved_prev)
        for earlier in range(block):
            partial_value = partial_value + product(lower_panel[block - 1, :, earlier, :], solved[earlier])
        residual = right_block[block] - partial_value
        solved.append(product(block_inverse[block], residual))
    return jnp.stack(solved)
```

```python
import functools

import jax
import jax.numpy as jnp
from jax import lax
from jax.experimental import pallas as pl
from jax.experimental.pallas import tpu as pltpu
from jax.sharding import PartitionSpec as P

F32, BF16 = jnp.float32, jnp.bfloat16
MESH = pl.DeviceIdType.MESH


def split(value):
    high = value.astype(BF16)
    return high, (value - high.astype(F32)).astype(BF16)


def product(left, both):
    high, low = split(left)
    n = both.shape[1] // 2
    wide = jnp.dot(high, both, preferred_element_type=F32)
    return wide[:, :n] + wide[:, n:] + jnp.dot(low, both[:, :n], preferred_element_type=F32)


def kernel(
    C, R, S,
    prev_hbm, lower_hbm, sprev_hbm, right_hbm, inv_hbm, out_ref,
    prev, lower, sprev, right, inv, sprev_both, part, from_l, from_r, to_l, to_r,
    xsend, xrecv, solved, acc,
    prev_sem, lower_sem, sprev_sem, right_sem, inv_sem,
    send_r, recv_l, send_l, recv_r, xs_sem, xr_sem,
):
    blocks, NR, _ = prev.shape
    NC = out_ref.shape[1]
    MH = part.shape[-1]
    CR = NR // S
    steps = 2 * blocks
    c, r = lax.axis_index("col"), lax.axis_index("row")
    has_l, has_r = c > 0, c < C - 1
    left, right_of = jnp.maximum(c - 1, 0), jnp.minimum(c + 1, C - 1)

    def rows(i):
        return pl.ds(pl.multiple_of(i * CR, CR), CR)

    def tri(k, j):
        return lax.div(k * (k - 1), 2) + j

    def load_prev(k):
        return pltpu.make_async_copy(prev_hbm.at[k], prev.at[k], prev_sem.at[k])

    def load_right(k):
        return pltpu.make_async_copy(right_hbm.at[k], right.at[k], right_sem.at[k])

    def load_inv(k, i):
        return pltpu.make_async_copy(inv_hbm.at[k, :, rows(i)], inv.at[k, i], inv_sem.at[k, i])

    def load_lower(k, j):
        return pltpu.make_async_copy(lower_hbm.at[k - 1, j], lower.at[tri(k, j)], lower_sem.at[tri(k, j)])

    def loop(n, body, start=0):
        lax.fori_loop(start, n, lambda i, _: (body(i), 0)[1], 0)

    load_sprev = pltpu.make_async_copy(sprev_hbm, sprev, sprev_sem)
    load_sprev.start()
    load_prev(0).start()
    load_right(0).start()
    loop(S, lambda i: load_inv(0, i).start())

    barrier = pltpu.get_barrier_semaphore()

    @pl.when(has_l)
    def _():
        pl.semaphore_signal(barrier, inc=1, device_id={"col": left}, device_id_type=MESH)

    @pl.when(has_r)
    def _():
        pl.semaphore_signal(barrier, inc=1, device_id={"col": right_of}, device_id_type=MESH)

    for d in range(1, R):
        pl.semaphore_signal(barrier, inc=1, device_id={"row": lax.rem(r + d, R)}, device_id_type=MESH)

    @pl.when(jnp.logical_not(has_l))
    def _():
        from_l[...] = jnp.zeros_like(from_l)

    @pl.when(jnp.logical_not(has_r))
    def _():
        from_r[...] = jnp.zeros_like(from_r)

    def push_right(p, i):
        return pltpu.make_async_remote_copy(
            src_ref=to_r.at[p, i], dst_ref=from_l.at[p, i],
            send_sem=send_r.at[p, i], recv_sem=recv_l.at[p, i],
            device_id={"col": right_of}, device_id_type=MESH)

    def push_left(p, i):
        return pltpu.make_async_remote_copy(
            src_ref=to_l.at[p, i], dst_ref=from_r.at[p, i],
            send_sem=send_l.at[p, i], recv_sem=recv_r.at[p, i],
            device_id={"col": left}, device_id_type=MESH)

    def push_x(slot, d):
        return pltpu.make_async_remote_copy(
            src_ref=xsend.at[slot], dst_ref=xrecv.at[slot, d - 1],
            send_sem=xs_sem.at[slot, d - 1], recv_sem=xr_sem.at[slot, d - 1],
            device_id={"row": lax.rem(r + d, R)}, device_id_type=MESH)

    def base(k, i):
        high, low = split(prev[k, rows(i), :])
        m = sprev_both.shape[1] // 2
        s_hi, s_lo = sprev_both[:, :m], sprev_both[:, m:]
        a = jnp.dot(high, s_hi, preferred_element_type=F32)
        a = a + jnp.dot(high, s_lo, preferred_element_type=F32)
        a = a + jnp.dot(low, s_hi, preferred_element_type=F32)
        value = jnp.where(has_l, 0.0, right[k, rows(i), :]) - a
        kp = lax.rem(k, 2)
        part[kp, 0, i] = value[:, :MH]
        part[kp, 1, i] = value[:, MH:]

    load_sprev.wait()
    m = sprev.shape[1]
    s_hi, s_lo = split(sprev[...])
    sprev_both[:, :m] = s_hi
    sprev_both[:, m:] = s_lo
    load_prev(0).wait()
    load_right(0).wait()
    pl.semaphore_wait(barrier, has_l.astype(jnp.int32) + has_r.astype(jnp.int32) + (R - 1))

    def consume(t):
        slot, k, h = lax.rem(t, 4), lax.div(t, 2), lax.rem(t, 2)
        total = xsend[slot]
        for d in range(1, R):
            push_x(slot, d).wait_recv()
            total = total + xrecv[slot, d - 1]
        for d in range(1, R):
            push_x(slot, d).wait_send()
        solved[k, h, :, :MH], solved[k, h, :, MH:] = split(total)

        @pl.when(h == 0)
        def _():
            out_ref[k, :, :MH] = total

        @pl.when(h == 1)
        def _():
            out_ref[k, :, MH:] = total

    def drain(p):
        def body(i):
            @pl.when(has_r)
            def _():
                push_right(p, i).wait_send()

            @pl.when(has_l)
            def _():
                push_left(p, i).wait_send()

        loop(S, body)

    def step(t):
        k, h = lax.div(t, 2), lax.rem(t, 2)
        kp, p, nk = lax.rem(k, 2), h, jnp.minimum(k + 1, blocks - 1)
        more = k < blocks - 1
        fresh = jnp.logical_and(h == 0, more)

        @pl.when(fresh)
        def _():
            load_prev(nk).start()
            load_right(nk).start()
            loop(k + 1, lambda j: load_lower(nk, j).start())
            loop(S, lambda i: load_inv(nk, i).start())

        def own(i):
            @pl.when(t == 0)
            def _():
                base(0, i)

            @pl.when(k > 0)
            def _():
                part[kp, h, i] -= product(lower[tri(k, k - 1), rows(i), :], solved[jnp.maximum(k - 1, 0), h])

            @pl.when(jnp.logical_not(has_l))
            def _():
                to_r[p, i] = part[kp, h, i]
                push_right(p, i).start()

            @pl.when(jnp.logical_not(has_r))
            def _():
                to_l[p, i] = part[kp, h, i]
                push_left(p, i).start()

        loop(S, own)

        @pl.when(fresh)
        def _():
            load_prev(nk).wait()
            load_right(nk).wait()
            loop(k + 1, lambda j: load_lower(nk, j).wait())

        def pass_right(i):
            @pl.when(has_l)
            def _():
                push_right(p, i).wait_recv()

                @pl.when(has_r)
                def _():
                    to_r[p, i] = from_l[p, i] + part[kp, h, i]
                    push_right(p, i).start()

        def pass_left(i):
            @pl.when(has_r)
            def _():
                push_left(p, i).wait_recv()

                @pl.when(has_l)
                def _():
                    to_l[p, i] = from_r[p, i] + part[kp, h, i]
                    push_left(p, i).start()

        def chunk(i):
            first = c < C // 2

            @pl.when(first)
            def _():
                pass_right(i)
                pass_left(i)

            @pl.when(jnp.logical_not(first))
            def _():
                pass_left(i)
                pass_right(i)

            @pl.when(h == 0)
            def _():
                load_inv(k, i).wait()

            high, low = split(from_l[p, i] + part[kp, h, i] + from_r[p, i])
            piece = product(inv[k, i], jnp.concatenate([high, low], axis=1))

            @pl.when(i == 0)
            def _():
                acc[...] = piece

            @pl.when(i > 0)
            def _():
                acc[...] += piece

            @pl.when(fresh)
            def _():
                base(nk, i)

            @pl.when(more)
            def _():
                def older(j):
                    part[1 - kp, h, i] -= product(lower[tri(nk, j), rows(i), :], solved[j, h])

                loop(k, older)

        loop(S, chunk)
        slot = lax.rem(t, 4)
        xsend[slot] = acc[...]
        for d in range(1, R):
            push_x(slot, d).start()

        @pl.when(t > 0)
        def _():
            consume(t - 1)
            drain(1 - p)

    loop(steps, step)
    consume(steps - 1)
    drain((steps - 1) % 2)


def local(C, R, prev_panel, lower_panel, solved_prev, right_block, block_inverse):
    blocks, NR, KP = prev_panel.shape
    M = solved_prev.shape[1]
    NC, MH = block_inverse.shape[1], M // 2
    S = max(1, min(4, NR // 128))
    CR = NR // S
    pairs = blocks * (blocks - 1) // 2
    dma = pltpu.SemaphoreType.DMA
    wide = pltpu.VMEM((2, S, CR, MH), F32)
    return pl.pallas_call(
        functools.partial(kernel, C, R, S),
        out_shape=jax.ShapeDtypeStruct((blocks, NC, M), F32),
        in_specs=[pl.BlockSpec(memory_space=pl.ANY)] * 5,
        out_specs=pl.BlockSpec(memory_space=pltpu.VMEM),
        scratch_shapes=[
            pltpu.VMEM((blocks, NR, KP), F32),
            pltpu.VMEM((pairs, NR, NC), F32),
            pltpu.VMEM((KP, M), F32),
            pltpu.VMEM((blocks, NR, M), F32),
            pltpu.VMEM((blocks, S, NC, CR), F32),
            pltpu.VMEM((KP, 2 * M), BF16),
            pltpu.VMEM((2, 2, S, CR, MH), F32),
            wide, wide, wide, wide,
            pltpu.VMEM((4, NC, MH), F32),
            pltpu.VMEM((4, max(R - 1, 1), NC, MH), F32),
            pltpu.VMEM((blocks, 2, NC, 2 * MH), BF16),
            pltpu.VMEM((NC, MH), F32),
            dma((blocks,)), dma((pairs,)), dma, dma((blocks,)), dma((blocks, S)),
            dma((2, S)), dma((2, S)), dma((2, S)), dma((2, S)),
            dma((4, max(R - 1, 1))), dma((4, max(R - 1, 1))),
        ],
        compiler_params=pltpu.CompilerParams(
            collective_id=0, has_side_effects=True, vmem_limit_bytes=63 * 2**20),
    )(prev_panel, jnp.transpose(lower_panel, (0, 2, 1, 3)), solved_prev, right_block, block_inverse)


def solution(mesh):
    return jax.shard_map(
        functools.partial(local, mesh.shape["col"], mesh.shape["row"]),
        mesh=mesh,
        in_specs=(
            P(None, "row", "col"),
            P(None, "row", None, "col"),
            P("col", ("groups", "rhs")),
            P("groups", "row", "rhs"),
            P(None, "col", "row"),
        ),
        out_specs=P("groups", "col", "rhs"),
        check_vma=False,
    )
```

```python
import functools

import jax
import jax.numpy as jnp
from jax import lax
from jax.experimental import pallas as pl
from jax.experimental.pallas import tpu as pltpu
from jax.sharding import PartitionSpec as P

F32, BF16 = jnp.float32, jnp.bfloat16
MESH = pl.DeviceIdType.MESH


def split(value):
    high = value.astype(BF16)
    return high, (value - high.astype(F32)).astype(BF16)


def product(left, both):
    high, low = split(left)
    n = both.shape[1] // 2
    wide = jnp.dot(high, both, preferred_element_type=F32)
    return wide[:, :n] + wide[:, n:] + jnp.dot(low, both[:, :n], preferred_element_type=F32)


def kernel(
    C, R, S, LAG, INJ,
    prev_hbm, lower_hbm, sprev_hbm, right_hbm, inv_hbm, out_ref,
    prev, lower, sprev, right, inv, sprev_both, part, from_l, from_r, to_l, to_r,
    xsend, xrecv, solved, acc,
    prev_sem, lower_sem, sprev_sem, right_sem, inv_sem,
    send_r, recv_l, send_l, recv_r, xs_sem, xr_sem,
):
    blocks, NR, _ = prev.shape
    NC = out_ref.shape[1]
    MH = part.shape[-1]
    CR = NR // S
    steps = 2 * blocks
    c, r = lax.axis_index("col"), lax.axis_index("row")
    has_l, has_r = c > 0, c < C - 1
    left, right_of = jnp.maximum(c - 1, 0), jnp.minimum(c + 1, C - 1)

    def rows(i):
        return pl.ds(pl.multiple_of(i * CR, CR), CR)

    def tri(k, j):
        return lax.div(k * (k - 1), 2) + j

    def load_prev(k):
        return pltpu.make_async_copy(prev_hbm.at[k], prev.at[k], prev_sem.at[k])

    def load_right(k):
        return pltpu.make_async_copy(right_hbm.at[k], right.at[k], right_sem.at[k])

    def load_inv(k, i):
        return pltpu.make_async_copy(inv_hbm.at[k, :, rows(i)], inv.at[k, i], inv_sem.at[k, i])

    def load_lower(k, j):
        return pltpu.make_async_copy(lower_hbm.at[k - 1, j], lower.at[tri(k, j)], lower_sem.at[tri(k, j)])

    def loop(n, body, start=0):
        lax.fori_loop(start, n, lambda i, _: (body(i), 0)[1], 0)

    load_sprev = pltpu.make_async_copy(sprev_hbm, sprev, sprev_sem)
    load_sprev.start()
    load_prev(0).start()
    load_right(0).start()
    loop(S, lambda i: load_inv(0, i).start())

    barrier = pltpu.get_barrier_semaphore()

    @pl.when(has_l)
    def _():
        pl.semaphore_signal(barrier, inc=1, device_id={"col": left}, device_id_type=MESH)

    @pl.when(has_r)
    def _():
        pl.semaphore_signal(barrier, inc=1, device_id={"col": right_of}, device_id_type=MESH)

    for d in range(1, R):
        pl.semaphore_signal(barrier, inc=1, device_id={"row": lax.rem(r + d, R)}, device_id_type=MESH)

    @pl.when(jnp.logical_not(has_l))
    def _():
        from_l[...] = jnp.zeros_like(from_l)

    @pl.when(jnp.logical_not(has_r))
    def _():
        from_r[...] = jnp.zeros_like(from_r)

    def push_right(p, i):
        return pltpu.make_async_remote_copy(
            src_ref=to_r.at[p, i], dst_ref=from_l.at[p, i],
            send_sem=send_r.at[p, i], recv_sem=recv_l.at[p, i],
            device_id={"col": right_of}, device_id_type=MESH)

    def push_left(p, i):
        return pltpu.make_async_remote_copy(
            src_ref=to_l.at[p, i], dst_ref=from_r.at[p, i],
            send_sem=send_l.at[p, i], recv_sem=recv_r.at[p, i],
            device_id={"col": left}, device_id_type=MESH)

    def push_x(slot, d):
        return pltpu.make_async_remote_copy(
            src_ref=xsend.at[slot], dst_ref=xrecv.at[slot, d - 1],
            send_sem=xs_sem.at[slot, d - 1], recv_sem=xr_sem.at[slot, d - 1],
            device_id={"row": lax.rem(r + d, R)}, device_id_type=MESH)

    def base(k, i):
        high, low = split(prev[k, rows(i), :])
        m = sprev_both.shape[1] // 2
        s_hi, s_lo = sprev_both[:, :m], sprev_both[:, m:]
        a = jnp.dot(high, s_hi, preferred_element_type=F32)
        a = a + jnp.dot(high, s_lo, preferred_element_type=F32)
        a = a + jnp.dot(low, s_hi, preferred_element_type=F32)
        value = jnp.where(has_l, 0.0, right[k, rows(i), :]) - a
        kp = lax.rem(k, 2)
        part[kp, 0, i] = value[:, :MH]
        part[kp, 1, i] = value[:, MH:]

    load_sprev.wait()
    m = sprev.shape[1]
    s_hi, s_lo = split(sprev[...])
    sprev_both[:, :m] = s_hi
    sprev_both[:, m:] = s_lo
    load_prev(0).wait()
    load_right(0).wait()
    pl.semaphore_wait(barrier, has_l.astype(jnp.int32) + has_r.astype(jnp.int32) + (R - 1))

    def consume(t):
        slot, k, h = lax.rem(t, 4), lax.div(t, 2), lax.rem(t, 2)
        total = xsend[slot]
        for d in range(1, R):
            push_x(slot, d).wait_recv()
            total = total + xrecv[slot, d - 1]
        for d in range(1, R):
            push_x(slot, d).wait_send()
        solved[k, h, :, :MH], solved[k, h, :, MH:] = split(total)

        @pl.when(h == 0)
        def _():
            out_ref[k, :, :MH] = total

        @pl.when(h == 1)
        def _():
            out_ref[k, :, MH:] = total

    def drain(p):
        def body(i):
            @pl.when(has_r)
            def _():
                push_right(p, i).wait_send()

            @pl.when(has_l)
            def _():
                push_left(p, i).wait_send()

        loop(S, body)

    def own(t, i):
        k, h = lax.div(t, 2), lax.rem(t, 2)
        kp, last = lax.rem(k, 2), jnp.maximum(k - 1, 0)

        @pl.when(k > 0)
        def _():
            part[kp, h, i] -= product(lower[tri(k, last), rows(i), :], solved[last, h])

        @pl.when(jnp.logical_not(has_l))
        def _():
            to_r[h, i] = part[kp, h, i]
            push_right(h, i).start()

        @pl.when(jnp.logical_not(has_r))
        def _():
            to_l[h, i] = part[kp, h, i]
            push_left(h, i).start()

    def step(t):
        k, p = lax.div(t, 2), lax.rem(t, 2)
        kp, nk = lax.rem(k, 2), jnp.minimum(k + 1, blocks - 1)
        more = k < blocks - 1
        fresh = jnp.logical_and(p == 0, more)

        @pl.when(fresh)
        def _():
            load_prev(nk).start()
            load_right(nk).start()
            loop(k + 1, lambda j: load_lower(nk, j).start())
            loop(S, lambda i: load_inv(nk, i).start())

        def pass_right(i):
            @pl.when(has_l)
            def _():
                push_right(p, i).wait_recv()

                @pl.when(has_r)
                def _():
                    to_r[p, i] = from_l[p, i] + part[kp, p, i]
                    push_right(p, i).start()

        def pass_left(i):
            @pl.when(has_r)
            def _():
                push_left(p, i).wait_recv()

                @pl.when(has_l)
                def _():
                    to_l[p, i] = from_r[p, i] + part[kp, p, i]
                    push_left(p, i).start()

        first = c < C // 2

        def either(flag, i):
            @pl.when(flag)
            def _():
                pass_right(i)

            @pl.when(jnp.logical_not(flag))
            def _():
                pass_left(i)

        def use(i):
            @pl.when(p == 0)
            def _():
                load_inv(k, i).wait()

            high, low = split(from_l[p, i] + part[kp, p, i] + from_r[p, i])
            piece = product(inv[k, i], jnp.concatenate([high, low], axis=1))

            @pl.when(i == 0)
            def _():
                acc[...] = piece

            @pl.when(i > 0)
            def _():
                acc[...] += piece

        def ahead(i):
            @pl.when(fresh)
            def _():
                @pl.when(i == 0)
                def _():
                    load_prev(nk).wait()
                    load_right(nk).wait()
                    loop(k + 1, lambda j: load_lower(nk, j).wait())

                base(nk, i)

            @pl.when(more)
            def _():
                def older(j):
                    part[1 - kp, p, i] -= product(lower[tri(nk, j), rows(i), :], solved[j, p])

                loop(k, older)

        def turn(n):
            @pl.when(n < S)
            def _():
                either(first, n)

            @pl.when(n >= LAG)
            def _():
                either(jnp.logical_not(first), n - LAG)

            @pl.when(n == INJ)
            def _():
                @pl.when(t > 0)
                def _():
                    consume(t - 1)
                    drain(1 - p)

                @pl.when(t < steps - 1)
                def _():
                    loop(S, lambda i: own(t + 1, i))

            @pl.when(n >= LAG)
            def _():
                use(n - LAG)
                ahead(n - LAG)

        loop(S + LAG, turn)
        slot = lax.rem(t, 4)
        xsend[slot] = acc[...]
        for d in range(1, R):
            push_x(slot, d).start()

    def begin(i):
        base(0, i)
        own(0, i)

    loop(S, begin)
    loop(steps, step)
    consume(steps - 1)
    drain((steps - 1) % 2)


def local(C, R, prev_panel, lower_panel, solved_prev, right_block, block_inverse):
    blocks, NR, KP = prev_panel.shape
    M = solved_prev.shape[1]
    NC, MH = block_inverse.shape[1], M // 2
    S = max(1, min(8, NR // 128))
    LAG = min(2, S - 1)
    INJ = max(LAG, S * 5 // 8)
    CR = NR // S
    pairs = blocks * (blocks - 1) // 2
    dma = pltpu.SemaphoreType.DMA
    wide = pltpu.VMEM((2, S, CR, MH), F32)
    return pl.pallas_call(
        functools.partial(kernel, C, R, S, LAG, INJ),
        out_shape=jax.ShapeDtypeStruct((blocks, NC, M), F32),
        in_specs=[pl.BlockSpec(memory_space=pl.ANY)] * 5,
        out_specs=pl.BlockSpec(memory_space=pltpu.VMEM),
        scratch_shapes=[
            pltpu.VMEM((blocks, NR, KP), F32),
            pltpu.VMEM((pairs, NR, NC), F32),
            pltpu.VMEM((KP, M), F32),
            pltpu.VMEM((blocks, NR, M), F32),
            pltpu.VMEM((blocks, S, NC, CR), F32),
            pltpu.VMEM((KP, 2 * M), BF16),
            pltpu.VMEM((2, 2, S, CR, MH), F32),
            wide, wide, wide, wide,
            pltpu.VMEM((4, NC, MH), F32),
            pltpu.VMEM((4, max(R - 1, 1), NC, MH), F32),
            pltpu.VMEM((blocks, 2, NC, 2 * MH), BF16),
            pltpu.VMEM((NC, MH), F32),
            dma((blocks,)), dma((pairs,)), dma, dma((blocks,)), dma((blocks, S)),
            dma((2, S)), dma((2, S)), dma((2, S)), dma((2, S)),
            dma((4, max(R - 1, 1))), dma((4, max(R - 1, 1))),
        ],
        compiler_params=pltpu.CompilerParams(
            collective_id=0, has_side_effects=True, vmem_limit_bytes=63 * 2**20),
    )(prev_panel, jnp.transpose(lower_panel, (0, 2, 1, 3)), solved_prev, right_block, block_inverse)


def solution(mesh):
    return jax.shard_map(
        functools.partial(local, mesh.shape["col"], mesh.shape["row"]),
        mesh=mesh,
        in_specs=(
            P(None, "row", "col"),
            P(None, "row", None, "col"),
            P("col", ("groups", "rhs")),
            P("groups", "row", "rhs"),
            P(None, "col", "row"),
        ),
        out_specs=P("groups", "col", "rhs"),
        check_vma=False,
    )
```

```python
import functools

import jax
import jax.numpy as jnp
from jax import lax
from jax.experimental import pallas as pl
from jax.experimental.pallas import tpu as pltpu
from jax.sharding import PartitionSpec as P

F32, BF16 = jnp.float32, jnp.bfloat16
MESH = pl.DeviceIdType.MESH


def split(value):
    high = value.astype(BF16)
    return high, (value - high.astype(F32)).astype(BF16)


def product(left, both):
    high, low = split(left)
    n = both.shape[1] // 2
    wide = jnp.dot(high, both, preferred_element_type=F32)
    return wide[:, :n] + wide[:, n:] + jnp.dot(low, both[:, :n], preferred_element_type=F32)


def kernel(
    C, R, S, G, LAG, INJ,
    prev_hbm, lower_hbm, sprev_hbm, right_hbm, inv_hbm, out_ref,
    prev, lower, sprev, right, inv, sprev_both, part, from_l, from_r, to_l, to_r,
    xsend, xrecv, solved, acc,
    prev_sem, lower_sem, sprev_sem, right_sem, inv_sem,
    send_r, recv_l, send_l, recv_r, xs_sem, xr_sem,
):
    blocks, NR, _ = prev.shape
    NC = out_ref.shape[1]
    MH = part.shape[-1]
    CR = NR // S
    Q, QR = S // G, CR * G
    steps = 2 * blocks
    c, r = lax.axis_index("col"), lax.axis_index("row")
    has_l, has_r = c > 0, c < C - 1
    left, right_of = jnp.maximum(c - 1, 0), jnp.minimum(c + 1, C - 1)

    def rows(q):
        return pl.ds(pl.multiple_of(q * QR, QR), QR)

    def group(q):
        return pl.ds(q * G, G)

    def tri(k, j):
        return lax.div(k * (k - 1), 2) + j

    def load_prev(k):
        return pltpu.make_async_copy(prev_hbm.at[k], prev.at[k], prev_sem.at[k])

    def load_right(k):
        return pltpu.make_async_copy(right_hbm.at[k], right.at[k], right_sem.at[k])

    def load_inv(k, i):
        return pltpu.make_async_copy(inv_hbm.at[k, :, rows(i)], inv.at[k, i], inv_sem.at[k, i])

    def load_lower(k, j):
        return pltpu.make_async_copy(lower_hbm.at[k - 1, j], lower.at[tri(k, j)], lower_sem.at[tri(k, j)])

    def loop(n, body, start=0):
        lax.fori_loop(start, n, lambda i, _: (body(i), 0)[1], 0)

    load_sprev = pltpu.make_async_copy(sprev_hbm, sprev, sprev_sem)
    load_sprev.start()
    load_prev(0).start()
    load_right(0).start()
    loop(Q, lambda q: load_inv(0, q).start())

    barrier = pltpu.get_barrier_semaphore()

    @pl.when(has_l)
    def _():
        pl.semaphore_signal(barrier, inc=1, device_id={"col": left}, device_id_type=MESH)

    @pl.when(has_r)
    def _():
        pl.semaphore_signal(barrier, inc=1, device_id={"col": right_of}, device_id_type=MESH)

    for d in range(1, R):
        pl.semaphore_signal(barrier, inc=1, device_id={"row": lax.rem(r + d, R)}, device_id_type=MESH)

    @pl.when(jnp.logical_not(has_l))
    def _():
        from_l[...] = jnp.zeros_like(from_l)

    @pl.when(jnp.logical_not(has_r))
    def _():
        from_r[...] = jnp.zeros_like(from_r)

    def push_right(p, i):
        return pltpu.make_async_remote_copy(
            src_ref=to_r.at[p, i], dst_ref=from_l.at[p, i],
            send_sem=send_r.at[p, i], recv_sem=recv_l.at[p, i],
            device_id={"col": right_of}, device_id_type=MESH)

    def push_left(p, i):
        return pltpu.make_async_remote_copy(
            src_ref=to_l.at[p, i], dst_ref=from_r.at[p, i],
            send_sem=send_l.at[p, i], recv_sem=recv_r.at[p, i],
            device_id={"col": left}, device_id_type=MESH)

    def push_x(slot, d):
        return pltpu.make_async_remote_copy(
            src_ref=xsend.at[slot], dst_ref=xrecv.at[slot, d - 1],
            send_sem=xs_sem.at[slot, d - 1], recv_sem=xr_sem.at[slot, d - 1],
            device_id={"row": lax.rem(r + d, R)}, device_id_type=MESH)

    def base(k, i):
        high, low = split(prev[k, rows(i), :])
        m = sprev_both.shape[1] // 2
        s_hi, s_lo = sprev_both[:, :m], sprev_both[:, m:]
        a = jnp.dot(high, s_hi, preferred_element_type=F32)
        a = a + jnp.dot(high, s_lo, preferred_element_type=F32)
        a = a + jnp.dot(low, s_hi, preferred_element_type=F32)
        value = jnp.where(has_l, 0.0, right[k, rows(i), :]) - a
        kp = lax.rem(k, 2)
        part[kp, 0, group(i)] = value[:, :MH].reshape(G, CR, MH)
        part[kp, 1, group(i)] = value[:, MH:].reshape(G, CR, MH)

    load_sprev.wait()
    m = sprev.shape[1]
    s_hi, s_lo = split(sprev[...])
    sprev_both[:, :m] = s_hi
    sprev_both[:, m:] = s_lo
    load_prev(0).wait()
    load_right(0).wait()
    pl.semaphore_wait(barrier, has_l.astype(jnp.int32) + has_r.astype(jnp.int32) + (R - 1))

    def consume(t):
        slot, k, h = lax.rem(t, 4), lax.div(t, 2), lax.rem(t, 2)
        total = xsend[slot]
        for d in range(1, R):
            push_x(slot, d).wait_recv()
            total = total + xrecv[slot, d - 1]
        for d in range(1, R):
            push_x(slot, d).wait_send()
        solved[k, h, :, :MH], solved[k, h, :, MH:] = split(total)

        @pl.when(h == 0)
        def _():
            out_ref[k, :, :MH] = total

        @pl.when(h == 1)
        def _():
            out_ref[k, :, MH:] = total

    def drain(p):
        def body(i):
            @pl.when(has_r)
            def _():
                push_right(p, i).wait_send()

            @pl.when(has_l)
            def _():
                push_left(p, i).wait_send()

        loop(S, body)

    def own(t, q):
        k, h = lax.div(t, 2), lax.rem(t, 2)
        kp, last = lax.rem(k, 2), jnp.maximum(k - 1, 0)

        @pl.when(k > 0)
        def _():
            less = product(lower[tri(k, last), rows(q), :], solved[last, h])
            part[kp, h, group(q)] -= less.reshape(G, CR, MH)

        @pl.when(jnp.logical_not(has_l))
        def _():
            to_r[h, group(q)] = part[kp, h, group(q)]
            for g in range(G):
                push_right(h, q * G + g).start()

        @pl.when(jnp.logical_not(has_r))
        def _():
            to_l[h, group(q)] = part[kp, h, group(q)]
            for g in range(G):
                push_left(h, q * G + g).start()

    def step(t):
        k, p = lax.div(t, 2), lax.rem(t, 2)
        kp, nk = lax.rem(k, 2), jnp.minimum(k + 1, blocks - 1)
        more = k < blocks - 1
        fresh = jnp.logical_and(p == 0, more)

        @pl.when(fresh)
        def _():
            load_prev(nk).start()
            load_right(nk).start()
            loop(k + 1, lambda j: load_lower(nk, j).start())
            loop(Q, lambda q: load_inv(nk, q).start())

        def pass_right(i):
            @pl.when(has_l)
            def _():
                push_right(p, i).wait_recv()

                @pl.when(has_r)
                def _():
                    to_r[p, i] = from_l[p, i] + part[kp, p, i]
                    push_right(p, i).start()

        def pass_left(i):
            @pl.when(has_r)
            def _():
                push_left(p, i).wait_recv()

                @pl.when(has_l)
                def _():
                    to_l[p, i] = from_r[p, i] + part[kp, p, i]
                    push_left(p, i).start()

        first = c < C // 2

        def either(flag, i):
            @pl.when(flag)
            def _():
                pass_right(i)

            @pl.when(jnp.logical_not(flag))
            def _():
                pass_left(i)

        def use(i):
            @pl.when(p == 0)
            def _():
                load_inv(k, i).wait()

            total = from_l[p, group(i)] + part[kp, p, group(i)] + from_r[p, group(i)]
            high, low = split(total.reshape(QR, MH))
            piece = product(inv[k, i], jnp.concatenate([high, low], axis=1))

            @pl.when(i == 0)
            def _():
                acc[...] = piece

            @pl.when(i > 0)
            def _():
                acc[...] += piece

        def ahead(i):
            @pl.when(fresh)
            def _():
                @pl.when(i == 0)
                def _():
                    load_prev(nk).wait()
                    load_right(nk).wait()
                    loop(k + 1, lambda j: load_lower(nk, j).wait())

                base(nk, i)

            @pl.when(more)
            def _():
                def older(j):
                    less = product(lower[tri(nk, j), rows(i), :], solved[j, p])
                    part[1 - kp, p, group(i)] -= less.reshape(G, CR, MH)

                loop(k, older)

        def turn(n):
            @pl.when(n < S)
            def _():
                either(first, n)

            @pl.when(n >= LAG)
            def _():
                either(jnp.logical_not(first), n - LAG)

            @pl.when(n == INJ)
            def _():
                @pl.when(t > 0)
                def _():
                    consume(t - 1)
                    drain(1 - p)

                @pl.when(t < steps - 1)
                def _():
                    loop(Q, lambda q: own(t + 1, q))

            @pl.when(jnp.logical_and(n >= LAG, lax.rem(n - LAG + 1, G) == 0))
            def _():
                q = lax.div(n - LAG, G)
                use(q)
                ahead(q)

        loop(S + LAG, turn)
        slot = lax.rem(t, 4)
        xsend[slot] = acc[...]
        for d in range(1, R):
            push_x(slot, d).start()

    def begin(i):
        base(0, i)
        own(0, i)

    loop(Q, begin)
    loop(steps, step)
    consume(steps - 1)
    drain((steps - 1) % 2)


def local(C, R, prev_panel, lower_panel, solved_prev, right_block, block_inverse):
    blocks, NR, KP = prev_panel.shape
    M = solved_prev.shape[1]
    NC, MH = block_inverse.shape[1], M // 2
    S = max(1, min(8, NR // 128))
    LAG = min(2, S - 1)
    INJ = max(LAG, S * 4 // 8)
    G = 2 if S % 2 == 0 else 1
    CR = NR // S
    pairs = blocks * (blocks - 1) // 2
    dma = pltpu.SemaphoreType.DMA
    wide = pltpu.VMEM((2, S, CR, MH), F32)
    return pl.pallas_call(
        functools.partial(kernel, C, R, S, G, LAG, INJ),
        out_shape=jax.ShapeDtypeStruct((blocks, NC, M), F32),
        in_specs=[pl.BlockSpec(memory_space=pl.ANY)] * 5,
        out_specs=pl.BlockSpec(memory_space=pltpu.VMEM),
        scratch_shapes=[
            pltpu.VMEM((blocks, NR, KP), F32),
            pltpu.VMEM((pairs, NR, NC), F32),
            pltpu.VMEM((KP, M), F32),
            pltpu.VMEM((blocks, NR, M), F32),
            pltpu.VMEM((blocks, S // G, NC, CR * G), F32),
            pltpu.VMEM((KP, 2 * M), BF16),
            pltpu.VMEM((2, 2, S, CR, MH), F32),
            wide, wide, wide, wide,
            pltpu.VMEM((4, NC, MH), F32),
            pltpu.VMEM((4, max(R - 1, 1), NC, MH), F32),
            pltpu.VMEM((blocks, 2, NC, 2 * MH), BF16),
            pltpu.VMEM((NC, MH), F32),
            dma((blocks,)), dma((pairs,)), dma, dma((blocks,)), dma((blocks, S // G)),
            dma((2, S)), dma((2, S)), dma((2, S)), dma((2, S)),
            dma((4, max(R - 1, 1))), dma((4, max(R - 1, 1))),
        ],
        compiler_params=pltpu.CompilerParams(
            collective_id=0, has_side_effects=True, vmem_limit_bytes=63 * 2**20),
    )(prev_panel, jnp.transpose(lower_panel, (0, 2, 1, 3)), solved_prev, right_block, block_inverse)


def solution(mesh):
    return jax.shard_map(
        functools.partial(local, mesh.shape["col"], mesh.shape["row"]),
        mesh=mesh,
        in_specs=(
            P(None, "row", "col"),
            P(None, "row", None, "col"),
            P("col", ("groups", "rhs")),
            P("groups", "row", "rhs"),
            P(None, "col", "row"),
        ),
        out_specs=P("groups", "col", "rhs"),
        check_vma=False,
    )
```
